128 devices in a mesh: row: 16 (over z, y), col: 8 (over x, core).
Axes of the slice: x: 4, y: 4, z: 4, core: 2. Of those that a mesh axis runs over, the one named last changes fastest.
Arguments:
- volume: bfloat16 [48, 128, 128, 128], P(None, ('row', 'col')), may hold values from -6 to 6
- norm_gain: float32 [2, 48], replicated, may hold values from 0.1 to 1.9
- in_proj: bfloat16 [2, 320, 48], replicated, may hold values from -0.875 to 0.875
- dt_proj: bfloat16 [2, 3, 48], replicated, may hold values from -0.875 to 0.875
- dt_bias: float32 [2, 3], replicated, may hold values from -2 to 1
- decay_rate: float32 [2, 3], replicated, may hold values from 2e-07 to 0.05
- conv_weight: float32 [2, 224, 4], replicated, may hold values from -3 to 3
- conv_bias: float32 [2, 224], replicated, may hold values from -3 to 3
- skip_gain: float32 [2, 3], replicated, may hold values from 0.5 to 1.5
- out_gain: float32 [2, 96], replicated, may hold values from 0.1 to 1.9
- out_proj: bfloat16 [2, 48, 96], replicated, may hold values from -0.625 to 0.625
- head_weight: bfloat16 [14, 48], replicated, may hold values from -2.6875 to 2.6875
- head_bias: float32 [14], replicated, may hold values from -6 to 6
- labels: int32 [128, 128, 128], P(('row', 'col')), may hold values from 0 to 13
- distance: int32 [14, 128, 128, 128], P(None, ('row', 'col')), may hold values from -16384 to 16384
Outputs:
- features: bfloat16 [48, 128, 128, 128], P(None, ('row', 'col'))
- logit_grad: float32 [14, 128, 128, 128], P(None, ('row', 'col'))
- total_loss: float32 [], replicated
The draws below stay inside these ranges and needn't reach their ends.
All inputs are finite; a program needn't handle non-finite values.
Results may differ from the reference program's by a relative error of at most 0.006.
The reference program's roundings to bfloat16 on the way count: a program that leaves them out, or rounds other values in their place, can miss the bound.
Values may be sent and summed in bfloat16 or wider, within the bound.
A program may use at most 192 MiB of HBM per device.

```python
import math
import jax
import jax.numpy as jnp
from jax import lax

D = 48
HEADS = 3
STATE = 64
CLASSES = 14
KERNEL = 4
SCAN_BLOCK = 128
BLOCKS = 2
YS = 128
INNER = 96
CONV_CH = 224
SIDE = 128
NTOT = 2097152


def place_ends(drawn, key, low, high):
    longest = drawn.shape.index(max(drawn.shape))
    spots = []
    for shift in (0, 1):
        where = [jax.random.randint(jax.random.fold_in(key, axis), (), 0, length) for axis, length in enumerate(drawn.shape)]
        where[longest] = (where[longest] + shift) % drawn.shape[longest]
        spots.append(tuple(where))
    return drawn.at[spots[0]].set(low).at[spots[1]].set(high)


def steps_of(stream_key, shape, split, least, high):
    def one(axis_at, blocks):
        heights = jax.random.uniform(jax.random.fold_in(jax.random.fold_in(stream_key, 6), axis_at), (blocks,), jnp.float32, least / len(split), high / len(split))
        return jnp.repeat(jnp.exp(heights), shape[axis_at] // blocks).reshape((-1,) + (1,) * (len(shape) - axis_at - 1))

    level = one(*split[0])
    for cut in split[1:]:
        level = level * one(*cut)
    return level


def scatter_about(rng, extent, width, bound, cuts=(), kind=jnp.bfloat16):
    array = width * jax.random.normal(rng, extent, jnp.float32)
    if cuts:
        array = array * steps_of(rng, extent, cuts, -0.22, 0.18)
    return jnp.clip(array, -bound, bound).astype(kind)


def setup_inputs(seed: int = 0) -> dict:
    keys = jax.random.split(jax.random.key(seed), 16)
    volume = scatter_about(keys[0], (D, SIDE, YS, SIDE), 1.0, 6.0, ((1, 128),))
    norm_gain = jnp.clip(1.0 + 0.18 * jax.random.normal(keys[1], (BLOCKS, D), jnp.float32), 0.1, 1.9)
    in_proj = scatter_about(keys[2], (BLOCKS, 2 * INNER + 2 * STATE, D), D ** -0.5, 0.875)
    dt_proj = scatter_about(keys[3], (BLOCKS, HEADS, D), D ** -0.5, 0.875)
    dt_bias = jnp.clip(jax.random.uniform(keys[4], (BLOCKS, HEADS), jnp.float32, -2.0, 1.0), -2.0, 1.0)
    decay_rate = jnp.clip(jnp.exp(jax.random.uniform(keys[5], (BLOCKS, HEADS), jnp.float32, math.log(2.0000000233721948e-07), math.log(0.05))), 2.0000000233721948e-07, 0.05)
    conv_weight = scatter_about(keys[6], (BLOCKS, CONV_CH, KERNEL), 0.5, 3.0, (), jnp.float32)
    conv_bias = scatter_about(keys[7], (BLOCKS, CONV_CH), 0.5, 3.0, (), jnp.float32)
    skip_gain = jnp.clip(jax.random.uniform(keys[8], (BLOCKS, HEADS), jnp.float32, 0.5, 1.5), 0.5, 1.5)
    out_gain = jnp.clip(1.0 + 0.18 * jax.random.normal(keys[9], (BLOCKS, INNER), jnp.float32), 0.1, 1.9)
    out_proj = scatter_about(keys[10], (BLOCKS, D, INNER), INNER ** -0.5, 0.625)
    head_weight = scatter_about(keys[11], (CLASSES, D), 0.45, 2.6875)
    head_bias = scatter_about(keys[12], (CLASSES,), 1.0, 6.0, (), jnp.float32)
    labels = place_ends(jax.random.randint(keys[13], (SIDE, SIDE, YS), 0, CLASSES), jax.random.fold_in(keys[13], 1), 0, CLASSES - 1).astype(jnp.int32)
    distance = place_ends(jax.random.randint(keys[14], (CLASSES, SIDE, SIDE, YS), -16384, 16385), jax.random.fold_in(keys[14], 1), -16384, 16384).astype(jnp.int32)
    return {"volume": volume, "norm_gain": norm_gain, "in_proj": in_proj, "dt_proj": dt_proj, "dt_bias": dt_bias, "decay_rate": decay_rate, "conv_weight": conv_weight, "conv_bias": conv_bias, "skip_gain": skip_gain, "out_gain": out_gain, "out_proj": out_proj, "head_weight": head_weight, "head_bias": head_bias, "labels": labels, "distance": distance}


eps = 1e-05
dist_unit = 4096.0
group_limit = 2048

def rms_scale(values, scale_gain):
    mean_sq = lax.optimization_barrier(jnp.mean(values * values, axis=0, keepdims=True))
    return values * lax.rsqrt(mean_sq + eps) * scale_gain[:, None]

def causal_conv(conv_in, tail_block, conv_weight, conv_bias):
    channels = conv_in.shape[0]
    tokens_here = conv_in.shape[1]
    span_count = tokens_here // SCAN_BLOCK
    tap_count = conv_weight.shape[1]
    blocks = conv_in.reshape(channels, span_count, SCAN_BLOCK)
    before = jnp.concatenate([tail_block[:, None, :], blocks[:, :-1]], axis=1)
    paired = jnp.concatenate([before, blocks], axis=2)
    source = lax.broadcasted_iota(jnp.int32, (2 * SCAN_BLOCK, SCAN_BLOCK), 0)
    target = lax.broadcasted_iota(jnp.int32, (2 * SCAN_BLOCK, SCAN_BLOCK), 1)
    conv_sum = jnp.zeros((channels, span_count, SCAN_BLOCK), jnp.float32) + conv_bias[:, None, None]
    for offset in range(tap_count):
        lag = tap_count - 1 - offset
        table = (source == target + SCAN_BLOCK - lag).astype(jnp.bfloat16)
        moved = jnp.einsum('cks,st->ckt', paired.astype(jnp.float32), table.astype(jnp.float32))
        conv_sum = conv_sum + conv_weight[:, offset:offset + 1, None] * moved
    return conv_sum.reshape(channels, tokens_here)

def local_pass(hidden_part, conv_tail, layer_params):
    norm_gain, in_proj, dt_proj, dt_bias, decay_rate, conv_weight, conv_bias, skip_gain, out_gain, out_proj = layer_params
    inner_width = out_proj.shape[1]
    head_count = decay_rate.shape[0]
    head_width = inner_width // head_count
    state_width = (in_proj.shape[0] - 2 * inner_width) // 2
    tokens_here = hidden_part.shape[1]
    span_count = tokens_here // SCAN_BLOCK
    normed = rms_scale(hidden_part.astype(jnp.float32), norm_gain).astype(jnp.bfloat16)
    projected = jnp.dot(in_proj, normed, preferred_element_type=jnp.float32).astype(jnp.bfloat16)
    dt_raw = jnp.dot(dt_proj, normed, preferred_element_type=jnp.float32)
    gate_part = projected[:inner_width]
    conv_in = projected[inner_width:]
    conv_sum = causal_conv(conv_in, conv_tail, conv_weight, conv_bias)
    conv_out = jax.nn.silu(conv_sum).astype(jnp.bfloat16)
    next_tail = conv_in[:, tokens_here - SCAN_BLOCK:]
    inner_values = conv_out[:inner_width]
    write_coef = conv_out[inner_width:inner_width + state_width]
    read_coef = conv_out[inner_width + state_width:]
    step_size = jax.nn.softplus(dt_raw + dt_bias[:, None])
    log_decay = -decay_rate[:, None] * step_size
    cum_decay = jnp.cumsum(log_decay.reshape(head_count, span_count, SCAN_BLOCK), axis=2)
    step_blocks = step_size.reshape(head_count, span_count, SCAN_BLOCK)
    write_blocks = write_coef.reshape(state_width, span_count, SCAN_BLOCK).astype(jnp.float32)
    read_blocks = read_coef.reshape(state_width, span_count, SCAN_BLOCK).astype(jnp.float32)
    scores = jnp.einsum('nkt,nks->kts', read_blocks, write_blocks)
    causal_mask = lax.broadcasted_iota(jnp.int32, (SCAN_BLOCK, SCAN_BLOCK), 0) >= lax.broadcasted_iota(jnp.int32, (SCAN_BLOCK, SCAN_BLOCK), 1)
    decay_gap = cum_decay[:, :, :, None] - cum_decay[:, :, None, :]
    decay_weight = jnp.exp(jnp.where(causal_mask, decay_gap, -jnp.inf))
    weights = (scores[None] * decay_weight * step_blocks[:, :, None, :]).astype(jnp.bfloat16)
    inner_heads = inner_values.reshape(head_count, head_width, span_count, SCAN_BLOCK)
    intra_out = jnp.einsum('hkts,hpks->hpkt', weights.astype(jnp.float32), inner_heads.astype(jnp.float32))
    local_out = intra_out + skip_gain[:, None, None, None] * inner_heads.astype(jnp.float32)
    block_decay = cum_decay[:, :, -1]
    carry_weight = jnp.exp(block_decay[:, :, None] - cum_decay) * step_blocks
    scaled_inner = (inner_heads.astype(jnp.float32) * carry_weight[:, None]).astype(jnp.bfloat16)
    block_state = jnp.einsum('hpkl,nkl->khpn', scaled_inner.astype(jnp.float32), write_blocks)
    return (next_tail, (local_out.reshape(inner_width, tokens_here), gate_part, read_coef, cum_decay, block_state, block_decay.T))

def finish_pass(hidden_part, local_out, gate_part, read_coef, cum_decay, entering, layer_params):
    norm_gain, in_proj, dt_proj, dt_bias, decay_rate, conv_weight, conv_bias, skip_gain, out_gain, out_proj = layer_params
    inner_width = out_proj.shape[1]
    head_count = decay_rate.shape[0]
    head_width = inner_width // head_count
    state_width = read_coef.shape[0]
    tokens_here = hidden_part.shape[1]
    span_count = tokens_here // SCAN_BLOCK
    read_blocks = read_coef.reshape(state_width, span_count, SCAN_BLOCK).astype(jnp.float32)
    inter_out = jnp.einsum('khpn,nkl->hpkl', entering.astype(jnp.float32), read_blocks)
    scan_out = local_out.reshape(head_count, head_width, span_count, SCAN_BLOCK) + jnp.exp(cum_decay)[:, None] * inter_out
    gated = scan_out.reshape(inner_width, tokens_here) * jax.nn.silu(gate_part.astype(jnp.float32))
    gated = rms_scale(gated, out_gain).astype(jnp.bfloat16)
    result = hidden_part.astype(jnp.float32) + jnp.dot(out_proj, gated, preferred_element_type=jnp.float32)
    return result.astype(jnp.bfloat16)

def mamba_layer(hidden, layer_params):
    model_width = hidden.shape[0]
    total_tokens = hidden.shape[1]
    group_size = min(group_limit, total_tokens)
    group_count = total_tokens // group_size
    conv_weight = layer_params[5]
    decay_rate = layer_params[4]
    out_proj = layer_params[9]
    head_count = decay_rate.shape[0]
    head_width = out_proj.shape[1] // head_count
    state_width = (layer_params[1].shape[0] - 2 * out_proj.shape[1]) // 2
    pieces = hidden.reshape(model_width, group_count, group_size).transpose(1, 0, 2)
    tail_start = jnp.zeros((conv_weight.shape[0], SCAN_BLOCK), jnp.bfloat16)
    state_start = jnp.zeros((head_count, head_width, state_width), jnp.float32)

    def group_step(carry, hidden_part):
        conv_tail, state_now = carry
        next_tail, parts = local_pass(hidden_part, conv_tail, layer_params)
        local_out, gate_part, read_coef, cum_decay, block_state, block_decay = parts

        def span_step(state_run, item):
            decay_now, contrib = item
            return (jnp.exp(decay_now)[:, None, None] * state_run + contrib, state_run)
        state_next, entering = lax.scan(span_step, state_now, (block_decay, block_state))
        result = finish_pass(hidden_part, local_out, gate_part, read_coef, cum_decay, entering.astype(jnp.bfloat16), layer_params)
        return ((next_tail, state_next), result)
    _, outputs = lax.scan(group_step, (tail_start, state_start), pieces)
    return outputs.transpose(1, 0, 2).reshape(model_width, total_tokens)

def reference(volume, norm_gain, in_proj, dt_proj, dt_bias, decay_rate, conv_weight, conv_bias, skip_gain, out_gain, out_proj, head_weight, head_bias, labels, distance):
    arrays = (norm_gain, in_proj, dt_proj, dt_bias, decay_rate, conv_weight, conv_bias, skip_gain, out_gain, out_proj)
    model_width = volume.shape[0]
    start_seq = volume.reshape(model_width, -1)
    after_first = mamba_layer(start_seq, tuple((entry[0] for entry in arrays)))
    relaid = after_first.reshape(model_width, SIDE, YS, SIDE).transpose(0, 3, 1, 2).reshape(model_width, -1)
    second = mamba_layer(relaid, tuple((entry[1] for entry in arrays)))
    features = second.reshape(model_width, SIDE, SIDE, YS)
    logits = jnp.dot(head_weight, second, preferred_element_type=jnp.float32) + head_bias[:, None]
    row_peak = lax.optimization_barrier(jnp.max(logits, axis=0, keepdims=True))
    shifted = jnp.exp(logits - row_peak)
    partition = lax.optimization_barrier(jnp.sum(shifted, axis=0, keepdims=True))
    probability = shifted / partition
    log_norm = row_peak[0] + jnp.log(partition[0])
    classes = logits.shape[0]
    one_hot = (labels.reshape(1, -1) == lax.broadcasted_iota(jnp.int32, (classes, 1), 0)).astype(jnp.float32)
    distance_map = distance.reshape(classes, -1).astype(jnp.float32) / dist_unit
    expect = lax.optimization_barrier(jnp.sum(probability * distance_map, axis=0))
    voxel_loss = log_norm - lax.optimization_barrier(jnp.sum(one_hot * logits, axis=0)) + expect
    logit_grad = probability - one_hot + probability * (distance_map - expect[None])
    x_index = lax.broadcasted_iota(jnp.int32, (SIDE, SIDE * YS), 0).astype(jnp.float32)
    voxel_weight = 1.0 + 3.0 * x_index / (SIDE - 1.0)
    total_loss = jnp.sum(voxel_weight * voxel_loss.reshape(SIDE, SIDE * YS)) / (2.5 * NTOT)
    return (features, logit_grad.reshape(classes, SIDE, SIDE, YS), total_loss)
```

```python
import functools

import jax
import jax.numpy as jnp
from jax import lax
from jax.experimental import pallas as pl
from jax.experimental.pallas import tpu as pltpu
from jax.sharding import PartitionSpec as P

LANES = 128
HEADS = 3
WIDTH = 32
INNER = 96
STATE = 64
CONV = 224
TAPS = 4
ROWS = 336
GROUP = 32
eps = 1e-05
dist_unit = 4096.0
LOG2E = 1.4426950408889634
AXES = ("row", "col")
f32 = jnp.float32
bf16 = jnp.bfloat16


def dot(a, b):
    return jnp.dot(a, b, preferred_element_type=f32)


def lane_index(shape):
    return lax.broadcasted_iota(jnp.int32, shape, len(shape) - 1)


def normalised(hidden, gain):
    x = hidden.astype(f32)
    mean_sq = jnp.mean(x * x, axis=0, keepdims=True)
    return (x * lax.rsqrt(mean_sq + eps) * gain).astype(bf16)


def per_head(rows):
    return jnp.concatenate([jnp.broadcast_to(rows[h : h + 1], (WIDTH, rows.shape[1])) for h in range(HEADS)], axis=0)


def local_body(
    unroll,
    h_ref,
    tail_ref,
    w_ref,
    gain_ref,
    taps_ref,
    dt_ref,
    skip_ref,
    tri_ref,
    local_ref,
    gate_ref,
    read_ref,
    cum_ref,
    block_ref,
    total_ref,
    log_ref,
    proj_ref,
    prev_ref,
    conv_ref,
    wide_ref,
):
    step_index = pl.program_id(0)

    @pl.when(step_index == 0)
    def _():
        before = dot(w_ref[...], normalised(tail_ref[...], gain_ref[...]))
        prev_ref[...] = before[INNER : INNER + CONV].astype(bf16).astype(f32)
        total_ref[...] = jnp.zeros_like(total_ref)
        log_ref[...] = jnp.zeros_like(log_ref)

    normed = jnp.concatenate([normalised(h_ref[u], gain_ref[...]) for u in range(unroll)], axis=1)
    proj_ref[...] = dot(w_ref[...], normed)

    dt_raw = proj_ref[INNER + CONV : INNER + CONV + 8, :]
    bias = jnp.concatenate([dt_ref[0]] * unroll, axis=1)
    rate = jnp.concatenate([dt_ref[1]] * unroll, axis=1)
    shifted = dt_raw + bias
    step = jnp.maximum(shifted, 0.0) + jnp.log1p(jnp.exp(-jnp.abs(shifted)))
    decay = -rate * step
    high = decay.astype(bf16).astype(f32)
    rest = decay - high
    mid = rest.astype(bf16).astype(f32)
    low = rest - mid
    parts = []
    for u in range(unroll):
        at = slice(u * LANES, (u + 1) * LANES)
        parts += [high[:, at], mid[:, at], low[:, at]]
    parts.append(jnp.zeros((8, LANES), f32))
    if len(parts) % 2:
        parts.append(jnp.zeros((8, LANES), f32))
    summed = dot(jnp.concatenate(parts, axis=0).astype(bf16), tri_ref[...])
    log_step = jnp.log(step) * LOG2E

    lane = lane_index((GROUP, LANES))
    for u in range(unroll):
        at = slice(u * LANES, (u + 1) * LANES)
        cum = (summed[24 * u + 16 : 24 * u + 24] + summed[24 * u + 8 : 24 * u + 16]) + summed[24 * u : 24 * u + 8]
        cum_ref[u] = cum
        less = cum - log_step[:, at]
        last = jnp.broadcast_to(cum[:, LANES - 1 : LANES], (8, LANES))
        carry_weight = jnp.exp2(last - less)

        gate_ref[u] = proj_ref[0:INNER, at].astype(bf16)
        for g in range(CONV // GROUP):
            rows = slice(g * GROUP, (g + 1) * GROUP)
            cur = proj_ref[INNER + g * GROUP : INNER + (g + 1) * GROUP, at].astype(bf16).astype(f32)
            prev = prev_ref[rows]
            half = taps_ref[TAPS, rows]
            for k in range(TAPS):
                lag = TAPS - 1 - k
                moved = cur
                if lag:
                    moved = pltpu.roll(jnp.where(lane >= LANES - lag, prev, cur), lag, axis=1)
                half = half + taps_ref[k, rows] * moved
            prev_ref[rows] = cur
            conv_ref[rows] = (half + half * jnp.tanh(half)).astype(bf16)

        inner = conv_ref[0:INNER]
        write = conv_ref[INNER : INNER + STATE]
        read = conv_ref[INNER + STATE :]
        read_ref[u] = read
        write_turned = write.astype(f32).T.astype(bf16)
        scores = dot(write_turned, read)
        source = lax.broadcasted_iota(jnp.int32, (LANES, LANES), 0)
        scores = jnp.where(source <= lane_index((LANES, LANES)), scores, 0.0)
        less_turned = less.T
        inner_wide = inner.astype(f32)
        for h in range(HEADS):
            rows = slice(h * WIDTH, (h + 1) * WIDTH)
            gap = cum[h : h + 1] - less_turned[:, h : h + 1]
            weights = (scores * jnp.exp2(jnp.minimum(gap, 126.0))).astype(bf16)
            local_ref[u, rows] = dot(inner[rows], weights) + skip_ref[rows] * inner_wide[rows]
        scaled = (inner_wide * per_head(carry_weight)).astype(bf16)
        state = dot(scaled, write_turned)
        block_ref[u] = state
        total_ref[...] = total_ref[...] * per_head(jnp.exp2(last))[:, :STATE] + state
        log_ref[...] = log_ref[...] + last


def finish_body(
    unroll,
    h_ref,
    local_ref,
    gate_ref,
    read_ref,
    cum_ref,
    block_ref,
    enter_ref,
    out_w_ref,
    gain_ref,
    result_ref,
    run_ref,
    gated_ref,
):
    @pl.when(pl.program_id(0) == 0)
    def _():
        run_ref[...] = enter_ref[...]

    for u in range(unroll):
        cum = cum_ref[u]
        running = run_ref[...]
        inter = dot(running.astype(bf16), read_ref[u])
        last = jnp.broadcast_to(cum[:, LANES - 1 : LANES], (8, LANES))
        run_ref[...] = running * per_head(jnp.exp2(last))[:, :STATE] + block_ref[u]
        scan = local_ref[u] + per_head(jnp.exp2(cum)) * inter
        half = 0.5 * gate_ref[u].astype(f32)
        gated = scan * (half + half * jnp.tanh(half))
        mean_sq = jnp.mean(gated * gated, axis=0, keepdims=True)
        gated_ref[:, u * LANES : (u + 1) * LANES] = (gated * lax.rsqrt(mean_sq + eps) * gain_ref[...]).astype(bf16)
    added = dot(out_w_ref[...], gated_ref[...])
    for u in range(unroll):
        result_ref[u] = (h_ref[u].astype(f32) + added[:, u * LANES : (u + 1) * LANES]).astype(bf16)


def whole(shape):
    return pl.BlockSpec(shape, lambda i: (0,) * len(shape))


def blocked(unroll, *rest):
    return pl.BlockSpec((unroll,) + rest, lambda i: (i,) + (0,) * len(rest))


def spread(values, width=LANES):
    return jnp.broadcast_to(values[..., None].astype(f32), values.shape + (width,))


def layer_tables(norm_gain, in_proj, dt_proj, dt_bias, decay_rate, conv_weight, conv_bias, skip_gain, out_gain, out_proj):
    weights = jnp.concatenate([in_proj, dt_proj, jnp.zeros((ROWS - in_proj.shape[0] - HEADS, in_proj.shape[1]), bf16)], axis=0)
    taps = spread(0.5 * jnp.concatenate([conv_weight.T, conv_bias[None]], axis=0))
    pad = jnp.zeros((8 - HEADS,), f32)
    dt_rows = spread(jnp.stack([jnp.concatenate([dt_bias, pad]), jnp.concatenate([decay_rate * LOG2E, pad])]))
    skip = spread(jnp.repeat(skip_gain, WIDTH))
    return weights, spread(norm_gain), taps, dt_rows, skip, spread(out_gain), out_proj


def local_call(hidden, tail, tables, unroll=4, interpret=False):
    blocks, model, _ = hidden.shape
    weights, gain, taps, dt_rows, skip, _, _ = tables
    tri = (lax.broadcasted_iota(jnp.int32, (LANES, LANES), 0) <= lax.broadcasted_iota(jnp.int32, (LANES, LANES), 1)).astype(bf16)
    shapes = (
        jax.ShapeDtypeStruct((blocks, INNER, LANES), f32),
        jax.ShapeDtypeStruct((blocks, INNER, LANES), bf16),
        jax.ShapeDtypeStruct((blocks, STATE, LANES), bf16),
        jax.ShapeDtypeStruct((blocks, 8, LANES), f32),
        jax.ShapeDtypeStruct((blocks, INNER, STATE), f32),
        jax.ShapeDtypeStruct((INNER, STATE), f32),
        jax.ShapeDtypeStruct((8, LANES), f32),
    )
    return pl.pallas_call(
        functools.partial(local_body, unroll),
        grid=(blocks // unroll,),
        out_shape=shapes,
        in_specs=[
            blocked(unroll, model, LANES),
            whole(tail.shape),
            whole(weights.shape),
            whole(gain.shape),
            whole(taps.shape),
            whole(dt_rows.shape),
            whole(skip.shape),
            whole(tri.shape),
        ],
        out_specs=[
            blocked(unroll, INNER, LANES),
            blocked(unroll, INNER, LANES),
            blocked(unroll, STATE, LANES),
            blocked(unroll, 8, LANES),
            blocked(unroll, INNER, STATE),
            whole((INNER, STATE)),
            whole((8, LANES)),
        ],
        scratch_shapes=[
            pltpu.VMEM((ROWS, unroll * LANES), f32),
            pltpu.VMEM((CONV, LANES), f32),
            pltpu.VMEM((CONV, LANES), bf16),
            pltpu.VMEM((8, LANES), f32),
        ],
        interpret=interpret,
        name="local_part",
    )(hidden, tail, weights, gain, taps, dt_rows, skip, tri)


def finish_call(hidden, parts, enter, tables, unroll=4, interpret=False):
    blocks, model, _ = hidden.shape
    local_out, gate, read, cum, block_state = parts
    out_gain, out_proj = tables[5:]
    return pl.pallas_call(
        functools.partial(finish_body, unroll),
        grid=(blocks // unroll,),
        out_shape=jax.ShapeDtypeStruct((blocks, model, LANES), bf16),
        in_specs=[
            blocked(unroll, model, LANES),
            blocked(unroll, INNER, LANES),
            blocked(unroll, INNER, LANES),
            blocked(unroll, STATE, LANES),
            blocked(unroll, 8, LANES),
            blocked(unroll, INNER, STATE),
            whole((INNER, STATE)),
            whole(out_proj.shape),
            whole(out_gain.shape),
        ],
        out_specs=blocked(unroll, model, LANES),
        scratch_shapes=[pltpu.VMEM((INNER, STATE), f32), pltpu.VMEM((INNER, unroll * LANES), bf16)],
        interpret=interpret,
        name="finish_part",
    )(hidden, local_out, gate, read, cum, block_state, enter, out_proj, out_gain)


def loss_body(
    x_size, block_z, second_ref, head_ref, bias_ref, label_ref, dist_ref, weight_ref, feat_ref, grad_ref, loss_ref, wide_ref, logit_ref
):
    @pl.when(pl.program_id(0) == 0)
    def _():
        loss_ref[...] = jnp.zeros_like(loss_ref)

    classes = dist_ref.shape[0]
    for z in range(block_z):
        block = second_ref[z]
        wide_ref[z] = block.astype(f32)
        logit_ref[z] = dot(head_ref[...], block) + bias_ref[...]
    for c in range(feat_ref.shape[0]):
        feat_ref[c] = wide_ref[:, c, :].astype(bf16)
    total = jnp.zeros((8, LANES), f32)
    for part in range(block_z // 8):
        at = slice(part * 8, (part + 1) * 8)
        logits = [logit_ref[at, k, :] for k in range(classes)]
        peak = functools.reduce(jnp.maximum, logits)
        shifted = [jnp.exp(v - peak) for v in logits]
        partition = functools.reduce(jnp.add, shifted)
        inverse = 1.0 / partition
        labels = label_ref[at]
        probability = [v * inverse for v in shifted]
        maps = [dist_ref[k, at, :].astype(f32) * (1.0 / dist_unit) for k in range(classes)]
        expect = functools.reduce(jnp.add, [p * m for p, m in zip(probability, maps)])
        hit = [labels == k for k in range(classes)]
        picked = functools.reduce(jnp.add, [jnp.where(m, v, 0.0) for m, v in zip(hit, logits)])
        total = total + (peak + jnp.log(partition)) - picked + expect
        for k in range(classes):
            grad_ref[k, at, :] = probability[k] - jnp.where(hit[k], 1.0, 0.0) + probability[k] * (maps[k] - expect)
    loss_ref[...] += total * weight_ref[...]


def loss_call(second, head_weight, head_bias, labels, distance, voxel_weight, block_z=16, interpret=False):
    planes, model, _ = second.shape
    classes = head_weight.shape[0]
    rows = 16
    head = jnp.concatenate([head_weight, jnp.zeros((rows - classes, model), bf16)], axis=0)
    bias = spread(jnp.concatenate([head_bias, jnp.zeros((rows - classes,), f32)]))
    return pl.pallas_call(
        functools.partial(loss_body, planes, block_z),
        grid=(planes // block_z,),
        out_shape=(
            jax.ShapeDtypeStruct((model, planes, LANES), bf16),
            jax.ShapeDtypeStruct((classes, planes, LANES), f32),
            jax.ShapeDtypeStruct((8, LANES), f32),
        ),
        in_specs=[
            blocked(block_z, model, LANES),
            whole(head.shape),
            whole(bias.shape),
            blocked(block_z, LANES),
            pl.BlockSpec((classes, block_z, LANES), lambda i: (0, i, 0)),
            whole((8, LANES)),
        ],
        out_specs=[
            pl.BlockSpec((model, block_z, LANES), lambda i: (0, i, 0)),
            pl.BlockSpec((classes, block_z, LANES), lambda i: (0, i, 0)),
            whole((8, LANES)),
        ],
        scratch_shapes=[pltpu.VMEM((block_z, model, LANES), f32), pltpu.VMEM((block_z, rows, LANES), f32)],
        interpret=interpret,
        name="loss_part",
    )(second, head, bias, labels, distance, jnp.broadcast_to(voxel_weight, (8, LANES)).astype(f32))


def passed_along(value):
    size = lax.axis_size(AXES)
    return lax.ppermute(value, AXES, [(i, i + 1) for i in range(size - 1)])


def entering_state(total, log):
    own = jnp.concatenate([total, log[:, :STATE]], axis=0)
    every = lax.all_gather(own, AXES)
    me = lax.axis_index(AXES)
    size = every.shape[0]
    logs = every[:, INNER : INNER + HEADS, 0]
    index = jnp.arange(size)
    between = (index[None, :] > index[:, None]) & (index[None, :] < me)
    gap = jnp.sum(jnp.where(between[:, :, None], logs[None], 0.0), axis=1)
    factor = jnp.where((index < me)[:, None], jnp.exp2(gap), 0.0)
    states = every[:, :INNER]
    return jnp.sum(jnp.repeat(factor, WIDTH, axis=1)[:, :, None] * states, axis=0)


def layer(hidden, params):
    tables = layer_tables(*params)
    tail = passed_along(hidden[-1])
    *parts, total, log = local_call(hidden, tail, tables)
    enter = entering_state(total, log)
    return finish_call(hidden, parts, enter, tables)


def per_device(
    volume,
    norm_gain,
    in_proj,
    dt_proj,
    dt_bias,
    decay_rate,
    conv_weight,
    conv_bias,
    skip_gain,
    out_gain,
    out_proj,
    head_weight,
    head_bias,
    labels,
    distance,
):
    arrays = (norm_gain, in_proj, dt_proj, dt_bias, decay_rate, conv_weight, conv_bias, skip_gain, out_gain, out_proj)
    model, _, cells_y, cells_x = volume.shape
    classes = head_weight.shape[0]
    hidden = volume.reshape(model, cells_y, cells_x).transpose(1, 0, 2)
    first = layer(hidden, tuple(entry[0] for entry in arrays))
    turned = first.transpose(2, 1, 0)
    relaid = lax.all_to_all(turned, AXES, split_axis=0, concat_axis=0, tiled=True)
    second = layer(relaid, tuple(entry[1] for entry in arrays))
    side = lax.axis_size(AXES)
    voxel_weight = 1.0 + 3.0 * lax.axis_index(AXES).astype(f32) / (side - 1.0)
    features, grad, loss = loss_call(
        second, head_weight, head_bias, labels.reshape(labels.shape[1:]), distance.reshape(classes, side, cells_y), voxel_weight
    )
    voxel_count = side * cells_y * side
    total_loss = lax.psum(jnp.sum(loss), AXES) / (2.5 * voxel_count)
    return features.reshape(model, 1, side, cells_y), grad.reshape(classes, 1, side, cells_y), total_loss


def solution(mesh):
    split = P(None, AXES, None, None)
    return jax.shard_map(
        per_device,
        mesh=mesh,
        in_specs=(split,) + (P(),) * 12 + (P(AXES, None, None), split),
        out_specs=(split, split, P()),
        check_vma=False,
    )
```
